32 devices in a mesh: seq: 4 (over y, core), exp: 8 (over z, x).
Axes of the slice: x: 2, y: 2, z: 4, core: 2. Of those that a mesh axis runs over, the one named last changes fastest.
Arguments:
- queries: bfloat16 [2048, 4096], P('seq', 'exp'), may hold values from -6 to 6
- key_rows: bfloat16 [2048, 512], P('seq', 'exp'), may hold values from -6 to 6
- value_rows: bfloat16 [2048, 512], P('seq', 'exp'), may hold values from -6 to 6
- sink_logits: float32 [64], P('exp'), may hold values from 0 to 6
- out_proj: bfloat16 [4096, 2560], P('exp'), may hold values from -0.09375 to 0.09375
- residual: bfloat16 [2048, 2560], P(('seq', 'exp')), may hold values from -0.59765625 to 0.59765625
- norm_gain: float32 [2560], replicated, may hold values from 0.25 to 1.75
- expert_ids: int32 [2048, 4], P(('seq', 'exp')), may hold values from 0 to 31, all different within a row; in each aligned block of 64 rows (0 to 63, 64 to 127, ...) at most 16 rows name the same one
- gate_weights: float32 [2048, 4], P(('seq', 'exp')), may hold values from 0.2 to 1
- w_gate_up: bfloat16 [32, 2560, 2880], P(('seq', 'exp')), may hold values from -0.125 to 0.125
- w_down: bfloat16 [32, 1440, 2560], P(('seq', 'exp')), may hold values from -0.15625 to 0.15625
Outputs:
- layer_out: bfloat16 [2048, 2560], P(('seq', 'exp'))
The draws below stay inside these ranges and needn't reach their ends.
Inputs may be any that keep to these rules, and one draw needn't show every extreme that they name: `expert_ids`: each row names 4 different experts. In the rows of one device (aligned blocks of 64 rows) no expert is named more than 16 times, and in every draw some expert is named exactly 16 times in some block.
All inputs are finite; a program needn't handle non-finite values.
Results may differ from the reference program's by a relative error of at most 0.022.
Values may be sent and summed in bfloat16 or wider, within the bound.
No kernel may reach another device: no remote copies, remote signals or barrier semaphores. Data moves between devices by JAX's collectives and lax.ppermute only.
A program may use at most 128 MiB of HBM per device.

```python
import math
import jax
import jax.numpy as jnp
import numpy as np
from jax import lax

D = 2560
FF_E = 1440
QH = 64
KVH = 8
HD = 64
WINDOW = 128
TOP = 4
TOKENS = 2048
TOK_DEV = 64
EXPERTS = 32
CAP = 16
N_EXP = 8


def draw_queries(key, part):
    drawn = jnp.clip(jax.random.normal(jax.random.fold_in(key, 1), (TOKENS, QH * HD), jnp.float32), -6.0, 6.0)
    return drawn.astype(jnp.bfloat16)


def draw_key_rows(key, part):
    drawn = jnp.clip(jax.random.normal(jax.random.fold_in(key, 2), (TOKENS, KVH * HD), jnp.float32), -6.0, 6.0)
    return drawn.astype(jnp.bfloat16)


def block_levels(stream_key, dims, pieces, low, largest):
    def one(position, parts):
        heights = jax.random.uniform(jax.random.fold_in(jax.random.fold_in(stream_key, 6), position), (parts,), jnp.float32, low / len(pieces), largest / len(pieces))
        return jnp.repeat(jnp.exp(heights), dims[position] // parts).reshape((-1,) + (1,) * (len(dims) - position - 1))

    factor_of = one(*pieces[0])
    for cut in pieces[1:]:
        factor_of = factor_of * one(*cut)
    return factor_of


def assign_block(stream_key, own, number, rows, amount, top, most, lean):
    sequence = jax.random.permutation(stream_key, amount)
    heavy_load, usual = portions_of(amount, rows * top, most, lean, True), portions_of(amount, rows * top, most, lean, False)
    places = jnp.arange(amount)

    def named(sizes, turn):
        used = int((sizes > 0).sum())
        fixed = max(1, used // 4)
        moved = fixed + (places - fixed + turn * (used - fixed)) % max(1, amount - fixed)
        return jnp.zeros((amount,), jnp.int32).at[sequence[jnp.where(places < fixed, places, moved)]].set(jnp.asarray(sizes, jnp.int32))

    sizes = jnp.where(number % 4 == 0, named(heavy_load, number // 4), named(usual, number - number // 4 - 1))
    mixed = jax.random.permutation(jax.random.fold_in(own, 3), amount)
    giver, taker = mixed[0:amount // 2 * 2:2], mixed[1:amount // 2 * 2:2]
    margin = jnp.minimum(sizes[giver] - 1, most - sizes[taker]) // 2
    margin = jnp.where((giver == sequence[0]) | (taker == sequence[0]) | (sizes[taker] == 0), 0, jnp.maximum(margin, 0))
    moved = jax.random.randint(jax.random.fold_in(own, 4), (amount // 2,), 0, 1 << 20) % (margin + 1)
    sizes = sizes.at[giver].add(-moved).at[taker].add(moved)
    labels = jnp.searchsorted(jnp.cumsum(sizes), jnp.arange(rows * top), side="right").astype(jnp.int32)
    grid = labels.reshape(top, rows).T
    grid = grid[jax.random.permutation(jax.random.fold_in(own, 1), rows)]
    turn = jax.random.randint(jax.random.fold_in(own, 2), (rows, 1), 0, top)
    return jnp.take_along_axis(grid, (jnp.arange(top)[None, :] + turn) % top, axis=1)


def portions_of(amount, total, bound, slope, full):
    weights = [(1 << 20) // math.isqrt(grade ** slope) + 1 for grade in range(1, amount + 1)]
    largest = bound if full else min(bound, max(-(-total // amount), total * weights[0] // sum(weights)))
    least = 1 if total - largest >= amount - 1 else 0
    given, spare = [largest] + [least] * (amount - 1), total - largest - least * (amount - 1)
    while spare > 0:
        candidates = [i for i in range(1, amount) if given[i] < largest] or [i for i in range(1, amount) if given[i] < bound]
        pool, budget = sum([weights[i] for i in candidates]), spare
        for i in candidates:
            addition = min(bound - given[i], max(1, budget * weights[i] // pool), spare)
            given[i] = given[i] + addition
            spare = spare - addition
    return np.array(given)


def gaussian(own_key, shape, scale, limit, pieces=(), kind=jnp.bfloat16):
    result = jax.random.normal(own_key, shape, jnp.float32) * scale
    if len(pieces) > 0:
        result = block_levels(own_key, shape, pieces, -0.22, 0.18) * result
    return jnp.clip(result, min=-limit, max=limit).astype(kind)


def setup_inputs(seed: int = 0) -> dict:
    keys = jax.random.split(jax.random.key(seed), 12)
    queries = draw_queries(jax.random.fold_in(keys[11], 71), 0)
    key_rows = draw_key_rows(jax.random.fold_in(keys[11], 71), 0)
    value_rows = gaussian(keys[2], (TOKENS, KVH * HD), 1.0, 6.0, ((0, 4), (1, 8)))
    sink_logits = jnp.clip(6.0 * jax.random.uniform(keys[3], (QH,), jnp.float32) ** block_levels(keys[3], (QH,), ((0, 8),), -0.2, 0.2), 0.0, 6.0)
    out_proj = gaussian(keys[4], (QH * HD, D), (QH * HD) ** -0.5, 0.09375, ((0, 8),))
    residual = gaussian(keys[5], (TOKENS, D), 0.1, 0.59765625, ((0, 32),))
    norm_gain = jnp.clip(1.0 + 0.15 * jax.random.normal(keys[6], (D,), jnp.float32), 0.25, 1.75)
    expert_ids_keys = jax.random.split(jax.random.fold_in(keys[7], 1), TOKENS // TOK_DEV)
    expert_ids_turns = jax.random.permutation(jax.random.fold_in(keys[7], 3), TOKENS // TOK_DEV)
    expert_ids = jax.vmap(lambda own, number: assign_block(jax.random.fold_in(keys[7], 2), own, number, TOK_DEV, EXPERTS, TOP, CAP, 2))(expert_ids_keys, expert_ids_turns).reshape((TOKENS, TOP))
    gate_weights = jnp.clip(0.2 + 0.8 * jax.random.uniform(keys[8], (TOKENS, TOP), jnp.float32) ** block_levels(keys[8], (TOKENS, TOP), ((0, 32),), -0.2, 0.2), 0.2, 1.0)
    w_gate_up = gaussian(keys[9], (EXPERTS, D, 2 * FF_E), D ** -0.5, 0.125, ((0, 32),))
    w_down = gaussian(keys[10], (EXPERTS, FF_E, D), FF_E ** -0.5, 0.15625, ((0, 32),))
    return {"queries": queries, "key_rows": key_rows, "value_rows": value_rows, "sink_logits": sink_logits, "out_proj": out_proj, "residual": residual, "norm_gain": norm_gain, "expert_ids": expert_ids, "gate_weights": gate_weights, "w_gate_up": w_gate_up, "w_down": w_down}


def window_attention(query_rows, key_block, value_block, prior_keys, prior_values, sink_row, first_index, window_size):
    row_count = query_rows.shape[0]
    head_width_dim = key_block.shape[1]
    head_count = query_rows.shape[1] // head_width_dim
    block_count = row_count // window_size
    key_ext = jnp.concatenate([prior_keys, key_block], axis=0)
    value_ext = jnp.concatenate([prior_values, value_block], axis=0)
    key_block_tiles = jnp.concatenate([key_ext[:row_count].reshape(block_count, window_size, head_width_dim), key_block.reshape(block_count, window_size, head_width_dim)], axis=1)
    value_block_tiles = jnp.concatenate([value_ext[:row_count].reshape(block_count, window_size, head_width_dim), value_block.reshape(block_count, window_size, head_width_dim)], axis=1)
    query_block_tiles = query_rows.reshape(block_count, window_size, head_count, head_width_dim)
    attention_scores = jnp.einsum('xnem,xcm->xenc', query_block_tiles.astype(jnp.float32), key_block_tiles.astype(jnp.float32)) * (1.0 / math.sqrt(head_width_dim))
    query_pos = jnp.arange(window_size, dtype=jnp.int32)[:, None]
    key_pos = jnp.arange(2 * window_size, dtype=jnp.int32)[None, :]
    inside = (key_pos > query_pos) & (key_pos <= query_pos + window_size)
    block_start = first_index + jnp.arange(block_count, dtype=jnp.int32) * window_size
    present = block_start[:, None] - window_size + key_pos >= 0
    allowed = inside[None, None, :, :] & present[:, None, None, :]
    attention_scores = jnp.where(allowed, attention_scores, -jnp.inf)
    sink_grid = sink_row.astype(jnp.float32)[None, :, None, None]
    highest = jnp.maximum(lax.optimization_barrier(jnp.max(attention_scores, axis=-1, keepdims=True)), sink_grid)
    raised = jnp.exp(attention_scores - highest)
    totals = lax.optimization_barrier(jnp.sum(raised, axis=-1, keepdims=True)) + jnp.exp(sink_grid - highest)
    attention_probabilities = (raised / totals).astype(jnp.bfloat16)
    mixed_value_rows = jnp.einsum('emjt,eta->ejma', attention_probabilities.astype(jnp.float32), value_block_tiles.astype(jnp.float32))
    return mixed_value_rows.astype(jnp.bfloat16).reshape(row_count, head_count * head_width_dim)

def expert_rows(rows_in, gate_up, down_rows):
    hidden_units = gate_up.shape[1] // 2
    both = jnp.dot(rows_in, gate_up, preferred_element_type=jnp.float32)
    gate_part = both[:, :hidden_units]
    up_part = both[:, hidden_units:]
    activated = (gate_part * jax.nn.sigmoid(1.702 * gate_part) * (up_part + 1.0)).astype(jnp.bfloat16)
    return jnp.dot(activated, down_rows, preferred_element_type=jnp.float32).astype(jnp.bfloat16)

def reference(queries, key_rows, value_rows, sink_logits, out_proj, residual, norm_gain, expert_ids, gate_weights, w_gate_up, w_down):
    total_rows = queries.shape[0]
    group_heads = QH // KVH
    query_heads = queries.reshape(total_rows, KVH, group_heads * HD).transpose(1, 0, 2)
    key_heads = key_rows.reshape(total_rows, KVH, HD).transpose(1, 0, 2)
    value_heads = value_rows.reshape(total_rows, KVH, HD).transpose(1, 0, 2)
    sink_heads = sink_logits.reshape(KVH, group_heads)
    prior_zero = jnp.zeros((WINDOW, HD), key_rows.dtype)

    def one_head(operands):
        return window_attention(operands[0], operands[1], operands[2], prior_zero, prior_zero, operands[3], 0, WINDOW)
    attended = lax.map(one_head, (query_heads, key_heads, value_heads, sink_heads))
    attended = attended.transpose(1, 0, 2).reshape(total_rows, QH * HD)
    group_width = QH * HD // N_EXP
    attn_groups = attended.reshape(total_rows, N_EXP, group_width).transpose(1, 0, 2)
    proj_groups = out_proj.reshape(N_EXP, group_width, D)

    def add_group(running, operands):
        partial_sum = jnp.dot(operands[0], operands[1], preferred_element_type=jnp.float32).astype(jnp.bfloat16)
        partial_sum = lax.optimization_barrier(partial_sum)
        return (running + partial_sum.astype(jnp.float32), None)
    projected = lax.scan(add_group, jnp.zeros((total_rows, D), jnp.float32), (attn_groups, proj_groups))[0]
    hidden = residual.astype(jnp.float32) + projected
    scale = lax.rsqrt(lax.optimization_barrier(jnp.mean(hidden * hidden, axis=-1, keepdims=True)) + 1e-05)
    normed = (hidden * scale * norm_gain.astype(jnp.float32)[None, :]).astype(jnp.bfloat16)
    flat_ids = expert_ids.reshape(-1).astype(jnp.int32)
    flat_gates = gate_weights.reshape(-1).astype(jnp.float32)
    capacity = EXPERTS * CAP
    token_of = (jnp.arange(flat_ids.shape[0], dtype=jnp.int32) // TOP).astype(jnp.int32)

    def expert_step(running, operands):
        expert_number, gate_up, down_rows = operands
        chosen = flat_ids == expert_number
        order = jnp.cumsum(chosen.astype(jnp.int32)) - 1
        slot_index = jnp.where(chosen, order, capacity).astype(jnp.int32)
        table = jnp.zeros((capacity,), jnp.int32).at[slot_index].set(token_of, mode='drop')
        slot_gates = jnp.zeros((capacity,), flat_gates.dtype).at[slot_index].set(flat_gates, mode='drop')
        outputs = expert_rows(normed[table], gate_up, down_rows)
        running = running.at[table].add(slot_gates[:, None] * outputs.astype(jnp.float32))
        return (running, None)
    combined = lax.scan(expert_step, hidden, (jnp.arange(EXPERTS, dtype=jnp.int32), w_gate_up, w_down))[0]
    return combined.astype(jnp.bfloat16)
```

```python
import math

import jax
import jax.numpy as jnp
from jax import lax
from jax.sharding import Mesh
from jax.sharding import PartitionSpec as P

KVH = 8
WINDOW = 128
SEQ = ("y", "c")
EXP = ("z", "x")


def factors(mesh):
    seq, exp = mesh.shape["seq"], mesh.shape["exp"]
    nc = 2 if seq % 2 == 0 else 1
    nz = 1
    while nz * nz < exp:
        nz *= 2
    return seq // nc, nc, nz, exp // nz


def swapped(value, axis, apart):
    return lax.ppermute(value, axis, [(i, i ^ 1 << apart) for i in range(lax.axis_size(axis))])


def shifted(block, axis, distance):
    devices = range(lax.axis_size(axis))
    route = [(i - distance, i) for i in devices if i - distance in devices]
    return lax.ppermute(block, axis, route)


def rotated(value, axis, by):
    size = lax.axis_size(axis)
    return lax.ppermute(value, axis, [(i, (i + by) % size) for i in range(size)])


def in_plane(value, dy, dx):
    ny, nx = lax.axis_size("y"), lax.axis_size("x")
    route = [
        (y * nx + x, (y + dy) % ny * nx + (x + dx) % nx) for y in range(ny) for x in range(nx)
    ]
    return lax.ppermute(value, ("y", "x"), route)


def window_attention(
    query_rows, key_block, value_block, prior_keys, prior_values, sink_row, first_index, window_size
):
    row_count = query_rows.shape[0]
    head_width_dim = key_block.shape[1]
    head_count = query_rows.shape[1] // head_width_dim
    block_count = row_count // window_size
    key_ext = jnp.concatenate([prior_keys, key_block], axis=0)
    value_ext = jnp.concatenate([prior_values, value_block], axis=0)
    key_block_tiles = jnp.concatenate(
        [
            key_ext[:row_count].reshape(block_count, window_size, head_width_dim),
            key_block.reshape(block_count, window_size, head_width_dim),
        ],
        axis=1,
    )
    value_block_tiles = jnp.concatenate(
        [
            value_ext[:row_count].reshape(block_count, window_size, head_width_dim),
            value_block.reshape(block_count, window_size, head_width_dim),
        ],
        axis=1,
    )
    query_block_tiles = query_rows.reshape(block_count, window_size, head_count, head_width_dim)
    attention_scores = jnp.einsum(
        "xnem,xcm->xenc", query_block_tiles, key_block_tiles, preferred_element_type=jnp.float32
    ) * (1.0 / math.sqrt(head_width_dim))
    query_pos = jnp.arange(window_size, dtype=jnp.int32)[:, None]
    key_pos = jnp.arange(2 * window_size, dtype=jnp.int32)[None, :]
    inside = (key_pos > query_pos) & (key_pos <= query_pos + window_size)
    block_start = first_index + jnp.arange(block_count, dtype=jnp.int32) * window_size
    present = block_start[:, None] - window_size + key_pos >= 0
    allowed = inside[None, None, :, :] & present[:, None, None, :]
    attention_scores = jnp.where(allowed, attention_scores, -jnp.inf)
    sink_grid = sink_row[None, :, None, None]
    highest = jnp.maximum(jnp.max(attention_scores, axis=-1, keepdims=True), sink_grid)
    raised = jnp.exp(attention_scores - highest)
    totals = jnp.sum(raised, axis=-1, keepdims=True) + jnp.exp(sink_grid - highest)
    attention_probabilities = (raised / totals).astype(jnp.bfloat16)
    mixed_value_rows = jnp.einsum(
        "emjt,eta->ejma",
        attention_probabilities,
        value_block_tiles,
        preferred_element_type=jnp.float32,
    )
    return mixed_value_rows.astype(jnp.bfloat16).reshape(row_count, head_count * head_width_dim)


def expert_rows(rows_in, gate_up, down_rows):
    hidden_units = gate_up.shape[1] // 2
    both = jnp.dot(rows_in, gate_up, preferred_element_type=jnp.float32)
    gate_part = both[:, :hidden_units]
    up_part = both[:, hidden_units:]
    activated = (gate_part * jax.nn.sigmoid(1.702 * gate_part) * (up_part + 1.0)).astype(
        jnp.bfloat16
    )
    return jnp.dot(activated, down_rows, preferred_element_type=jnp.float32).astype(jnp.bfloat16)


def per_device(
    queries,
    key_rows,
    value_rows,
    sink_logits,
    out_proj,
    residual,
    norm_gain,
    expert_ids,
    gate_weights,
    w_gate_up,
    w_down,
):
    f32, bf16 = jnp.float32, jnp.bfloat16
    ny, nc, nz, nx = (lax.axis_size(a) for a in ("y", "c", "z", "x"))
    yi, ci, zi, xi = (lax.axis_index(a) for a in ("y", "c", "z", "x"))
    seq_index = yi * nc + ci
    exp_index = zi * nx + xi
    local_rows = queries.shape[0]
    width = out_proj.shape[1]
    tokens = local_rows // (nz * nx)
    expert_total = ny * nc * nz * nx
    top_count = expert_ids.shape[1]
    cap = 2 * top_count * tokens // expert_total

    group_devices = nz * nx // KVH
    key_piece = key_rows
    value_piece = value_rows
    for bit_number in range(group_devices.bit_length() - 1):
        other_keys, other_values = swapped((key_piece, value_piece), EXP, bit_number)
        upper_half = jnp.right_shift(exp_index, bit_number) & 1 == 1
        key_piece = jnp.where(
            upper_half,
            jnp.concatenate([other_keys, key_piece], axis=1),
            jnp.concatenate([key_piece, other_keys], axis=1),
        )
        value_piece = jnp.where(
            upper_half,
            jnp.concatenate([other_values, value_piece], axis=1),
            jnp.concatenate([value_piece, other_values], axis=1),
        )
    prior_keys, prior_values = shifted(
        (key_piece[local_rows - WINDOW :], value_piece[local_rows - WINDOW :]), SEQ, 1
    )

    flat_ids = expert_ids.reshape(-1)
    chosen = (flat_ids[:, None] == jnp.arange(expert_total, dtype=jnp.int32)[None, :]).astype(
        jnp.int32
    )
    slot_rank = jnp.sum((jnp.cumsum(chosen, axis=0) - chosen) * chosen, axis=1)
    slot_index = (flat_ids * cap + slot_rank).reshape(tokens, top_count)
    facts = jnp.concatenate([slot_index.astype(f32), gate_weights], axis=1)
    facts_of = [facts] + [rotated(facts, "z", k) for k in range(1, nz)]

    places = jnp.arange(ny * nx * nc * cap, dtype=jnp.int32)
    rank, rest = places % cap, places // cap
    to_c, rest = (ci + rest % nc) % nc, rest // nc
    to_x, to_y = (xi + rest % nx) % nx, (yi + rest // nx) % ny
    plane_slots = (((to_y * nc + to_c) * nz + zi) * nx + to_x) * cap + rank
    plane_rows = ny * nx * nc * cap

    attended = window_attention(
        queries,
        key_piece,
        value_piece,
        prior_keys,
        prior_values,
        sink_logits,
        seq_index * local_rows,
        WINDOW,
    )
    partial = jnp.dot(attended, out_proj, preferred_element_type=f32).astype(bf16)

    def rows_of(z, x):
        return lax.dynamic_slice(partial, ((z % nz * nx + x % nx) * tokens, 0), (tokens, width))

    crossed = []
    for step in range(nz):
        block = zi - 1 - step + 2 * nz
        crossed.append(
            [rotated(rows_of(block, xi + dx), "x", dx) for dx in range(1, nx)]
            + [rows_of(block, xi)]
        )
    running = None
    for step in range(nz):
        total = sum(piece.astype(f32) for piece in crossed[step])
        if running is not None:
            total = total + rotated(running, "z", 1).astype(f32)
        running = total.astype(bf16)
    hidden = residual.astype(f32) + total
    scale = lax.rsqrt(jnp.mean(hidden * hidden, axis=-1, keepdims=True) + 1e-05)
    normed = (hidden * scale * norm_gain[None, :]).astype(bf16)

    offsets = [(dy, dx) for dy in range(ny) for dx in range(nx)]
    arriving = normed
    inputs = []
    spreads = []
    for k in range(nz):
        if k:
            arriving = rotated(arriving, "z", 1)
        slots = facts_of[k][:, :top_count].astype(jnp.int32)
        hits = plane_slots[None, None, :] == slots[:, :, None]
        spread = jnp.sum(jnp.where(hits, facts_of[k][:, top_count:, None], 0.0), axis=1)
        spreads.append(spread)
        placing = jnp.any(hits, axis=1).astype(bf16)
        placed = lax.dot_general(
            placing, arriving, (((0,), (0,)), ((), ())), preferred_element_type=f32
        ).astype(bf16)
        placed = placed.reshape(ny * nx, nc, cap, width)
        here = jnp.stack(
            [placed[0]] + [in_plane(placed[j], *offsets[j]) for j in range(1, ny * nx)]
        )
        inputs.append(
            [here[:, 0]] + [rotated(here[:, dc], "c", dc) for dc in range(1, nc)]
        )
    rows_in = jnp.stack([jnp.stack(parts) for parts in inputs])
    results = expert_rows(rows_in.reshape(nz * plane_rows, width), w_gate_up[0], w_down[0])
    results = results.reshape(nz, nc, ny * nx, cap, width)

    running = None
    for k in list(range(1, nz)) + [0]:
        back = jnp.stack(
            [results[k, 0]] + [rotated(results[k, dc], "c", -dc) for dc in range(1, nc)], axis=1
        )
        rows_back = jnp.stack(
            [back[0]]
            + [in_plane(back[j], -offsets[j][0], -offsets[j][1]) for j in range(1, ny * nx)]
        ).reshape(plane_rows, width)
        high = spreads[k].astype(bf16)
        low = (spreads[k] - high.astype(f32)).astype(bf16)
        total = jnp.dot(high, rows_back, preferred_element_type=f32) + jnp.dot(
            low, rows_back, preferred_element_type=f32
        )
        if running is not None:
            total = total + rotated(running, "z", 1).astype(f32)
        running = total.astype(bf16)
    return (hidden + total).astype(bf16)


def solution(mesh):
    sizes = factors(mesh)
    inner = Mesh(mesh.devices.reshape(sizes), ("y", "c", "z", "x"))
    every = SEQ + EXP
    return jax.shard_map(
        per_device,
        mesh=inner,
        in_specs=(
            P(SEQ, EXP),
            P(SEQ, EXP),
            P(SEQ, EXP),
            P(EXP),
            P(EXP, None),
            P(every, None),
            P(),
            P(every, None),
            P(every, None),
            P(every, None, None),
            P(every, None, None),
        ),
        out_specs=P(every, None),
        check_vma=False,
    )
```

```python
import math

import jax
import jax.numpy as jnp
from jax import lax
from jax.sharding import Mesh
from jax.sharding import PartitionSpec as P

KVH = 8
WINDOW = 128
SEQ = ("y", "c")
EXP = ("z", "x")


def factors(mesh):
    seq, exp = mesh.shape["seq"], mesh.shape["exp"]
    nc = 2 if seq % 2 == 0 else 1
    nz = 1
    while nz * nz < exp:
        nz *= 2
    return seq // nc, nc, nz, exp // nz


def swapped(value, axis, apart):
    return lax.ppermute(value, axis, [(i, i ^ 1 << apart) for i in range(lax.axis_size(axis))])


def shifted(block, axis, distance):
    devices = range(lax.axis_size(axis))
    route = [(i - distance, i) for i in devices if i - distance in devices]
    return lax.ppermute(block, axis, route)


def rotated(value, axis, by):
    size = lax.axis_size(axis)
    return lax.ppermute(value, axis, [(i, (i + by) % size) for i in range(size)])


def in_plane(value, dy, dx):
    ny, nx = lax.axis_size("y"), lax.axis_size("x")
    route = [
        (y * nx + x, (y + dy) % ny * nx + (x + dx) % nx) for y in range(ny) for x in range(nx)
    ]
    return lax.ppermute(value, ("y", "x"), route)


def window_attention(
    query_rows, key_block, value_block, prior_keys, prior_values, sink_row, first_index, window_size
):
    row_count = query_rows.shape[0]
    head_width_dim = key_block.shape[1]
    head_count = query_rows.shape[1] // head_width_dim
    block_count = row_count // window_size
    key_ext = jnp.concatenate([prior_keys, key_block], axis=0)
    value_ext = jnp.concatenate([prior_values, value_block], axis=0)
    key_block_tiles = jnp.concatenate(
        [
            key_ext[:row_count].reshape(block_count, window_size, head_width_dim),
            key_block.reshape(block_count, window_size, head_width_dim),
        ],
        axis=1,
    )
    value_block_tiles = jnp.concatenate(
        [
            value_ext[:row_count].reshape(block_count, window_size, head_width_dim),
            value_block.reshape(block_count, window_size, head_width_dim),
        ],
        axis=1,
    )
    query_block_tiles = query_rows.reshape(block_count, window_size, head_count, head_width_dim)
    attention_scores = jnp.einsum(
        "xnem,xcm->xenc", query_block_tiles, key_block_tiles, preferred_element_type=jnp.float32
    ) * (1.0 / math.sqrt(head_width_dim))
    query_pos = jnp.arange(window_size, dtype=jnp.int32)[:, None]
    key_pos = jnp.arange(2 * window_size, dtype=jnp.int32)[None, :]
    inside = (key_pos > query_pos) & (key_pos <= query_pos + window_size)
    block_start = first_index + jnp.arange(block_count, dtype=jnp.int32) * window_size
    present = block_start[:, None] - window_size + key_pos >= 0
    allowed = inside[None, None, :, :] & present[:, None, None, :]
    attention_scores = jnp.where(allowed, attention_scores, -jnp.inf)
    sink_grid = sink_row[None, :, None, None]
    highest = jnp.maximum(jnp.max(attention_scores, axis=-1, keepdims=True), sink_grid)
    raised = jnp.exp(attention_scores - highest)
    totals = jnp.sum(raised, axis=-1, keepdims=True) + jnp.exp(sink_grid - highest)
    attention_probabilities = (raised / totals).astype(jnp.bfloat16)
    mixed_value_rows = jnp.einsum(
        "emjt,eta->ejma",
        attention_probabilities,
        value_block_tiles,
        preferred_element_type=jnp.float32,
    )
    return mixed_value_rows.astype(jnp.bfloat16).reshape(row_count, head_count * head_width_dim)


def expert_rows(rows_in, gate_up, down_rows):
    hidden_units = gate_up.shape[1] // 2
    both = jnp.dot(rows_in, gate_up, preferred_element_type=jnp.float32)
    gate_part = both[:, :hidden_units]
    up_part = both[:, hidden_units:]
    activated = (gate_part * jax.nn.sigmoid(1.702 * gate_part) * (up_part + 1.0)).astype(
        jnp.bfloat16
    )
    return jnp.dot(activated, down_rows, preferred_element_type=jnp.float32).astype(jnp.bfloat16)


def per_device(
    queries,
    key_rows,
    value_rows,
    sink_logits,
    out_proj,
    residual,
    norm_gain,
    expert_ids,
    gate_weights,
    w_gate_up,
    w_down,
):
    f32, bf16 = jnp.float32, jnp.bfloat16
    ny, nc, nz, nx = (lax.axis_size(a) for a in ("y", "c", "z", "x"))
    yi, ci, zi, xi = (lax.axis_index(a) for a in ("y", "c", "z", "x"))
    seq_index = yi * nc + ci
    exp_index = zi * nx + xi
    local_rows = queries.shape[0]
    width = out_proj.shape[1]
    tokens = local_rows // (nz * nx)
    expert_total = ny * nc * nz * nx
    top_count = expert_ids.shape[1]
    cap = 2 * top_count * tokens // expert_total

    group_devices = nz * nx // KVH
    key_piece = key_rows
    value_piece = value_rows
    for bit_number in range(group_devices.bit_length() - 1):
        other_keys, other_values = swapped((key_piece, value_piece), EXP, bit_number)
        upper_half = jnp.right_shift(exp_index, bit_number) & 1 == 1
        key_piece = jnp.where(
            upper_half,
            jnp.concatenate([other_keys, key_piece], axis=1),
            jnp.concatenate([key_piece, other_keys], axis=1),
        )
        value_piece = jnp.where(
            upper_half,
            jnp.concatenate([other_values, value_piece], axis=1),
            jnp.concatenate([value_piece, other_values], axis=1),
        )
    prior_keys, prior_values = shifted(
        (key_piece[local_rows - WINDOW :], value_piece[local_rows - WINDOW :]), SEQ, 1
    )

    flat_ids = expert_ids.reshape(-1)
    chosen = (flat_ids[:, None] == jnp.arange(expert_total, dtype=jnp.int32)[None, :]).astype(
        jnp.int32
    )
    slot_rank = jnp.sum((jnp.cumsum(chosen, axis=0) - chosen) * chosen, axis=1)
    slot_index = (flat_ids * cap + slot_rank).reshape(tokens, top_count)
    facts = jnp.concatenate([slot_index.astype(f32), gate_weights], axis=1)
    facts_of = [facts] + [rotated(facts, "z", k) for k in range(1, nz)]

    places = jnp.arange(ny * nx * nc * cap, dtype=jnp.int32)
    rank, rest = places % cap, places // cap
    to_c, rest = (ci + rest % nc) % nc, rest // nc
    to_x, to_y = (xi + rest % nx) % nx, (yi + rest // nx) % ny
    plane_slots = (((to_y * nc + to_c) * nz + zi) * nx + to_x) * cap + rank
    plane_rows = ny * nx * nc * cap

    attended = window_attention(
        queries,
        key_piece,
        value_piece,
        prior_keys,
        prior_values,
        sink_logits,
        seq_index * local_rows,
        WINDOW,
    )
    partial = jnp.dot(attended, out_proj, preferred_element_type=f32).astype(bf16)

    def rows_of(z, x):
        return lax.dynamic_slice(partial, ((z % nz * nx + x % nx) * tokens, 0), (tokens, width))

    crossed = []
    for step in range(nz):
        block = zi - 1 - step + 2 * nz
        crossed.append(
            [rotated(rows_of(block, xi + dx), "x", dx) for dx in range(1, nx)]
            + [rows_of(block, xi)]
        )
    running = None
    for step in range(nz):
        total = sum(piece.astype(f32) for piece in crossed[step])
        if running is not None:
            total = total + rotated(running, "z", 1).astype(f32)
        running = total.astype(bf16)
    hidden = residual.astype(f32) + total
    scale = lax.rsqrt(jnp.mean(hidden * hidden, axis=-1, keepdims=True) + 1e-05)
    normed = (hidden * scale * norm_gain[None, :]).astype(bf16)

    offsets = [(dy, dx) for dy in range(ny) for dx in range(nx)]
    arriving = normed
    landed = []
    spreads = []
    for k in range(nz):
        if k:
            arriving = rotated(arriving, "z", 1)
        slots = facts_of[k][:, :top_count].astype(jnp.int32)
        hits = plane_slots[None, None, :] == slots[:, :, None]
        spread = jnp.sum(jnp.where(hits, facts_of[k][:, top_count:, None], 0.0), axis=1)
        spreads.append(spread)
        placing = jnp.any(hits, axis=1).astype(bf16)
        placed = lax.dot_general(
            placing, arriving, (((0,), (0,)), ((), ())), preferred_element_type=f32
        ).astype(bf16)
        placed = placed.reshape(ny * nx, nc, cap, width)
        landed.append(
            jnp.stack([placed[0]] + [in_plane(placed[j], *offsets[j]) for j in range(1, ny * nx)])
        )

    groups = [list(range(min(2, nz)))] + [[k] for k in range(2, nz)]
    returned = [None] * nz
    for group in groups:
        mine = jnp.stack([landed[k][:, 0] for k in group])
        given = [mine]
        for dc in range(1, nc):
            given.append(rotated(jnp.stack([landed[k][:, dc] for k in group]), "c", dc))
        rows_in = jnp.stack(given)
        results = expert_rows(rows_in.reshape(-1, width), w_gate_up[0], w_down[0])
        results = results.reshape(rows_in.shape)
        back = [results[0]]
        for dc in range(1, nc):
            back.append(rotated(results[dc], "c", -dc))
        for i, k in enumerate(group):
            returned[k] = jnp.stack([part[i] for part in back], axis=1)

    running = None
    for k in list(range(1, nz)) + [0]:
        rows_back = jnp.stack(
            [returned[k][0]]
            + [in_plane(returned[k][j], -offsets[j][0], -offsets[j][1]) for j in range(1, ny * nx)]
        ).reshape(plane_rows, width)
        high = spreads[k].astype(bf16)
        low = (spreads[k] - high.astype(f32)).astype(bf16)
        total = jnp.dot(high, rows_back, preferred_element_type=f32) + jnp.dot(
            low, rows_back, preferred_element_type=f32
        )
        if running is not None:
            total = total + rotated(running, "z", 1).astype(f32)
        running = total.astype(bf16)
    return (hidden + total).astype(bf16)


def solution(mesh):
    sizes = factors(mesh)
    inner = Mesh(mesh.devices.reshape(sizes), ("y", "c", "z", "x"))
    every = SEQ + EXP

    return jax.shard_map(
        per_device,
        mesh=inner,
        in_specs=(
            P(SEQ, EXP),
            P(SEQ, EXP),
            P(SEQ, EXP),
            P(EXP),
            P(EXP, None),
            P(every, None),
            P(),
            P(every, None),
            P(every, None),
            P(every, None, None),
            P(every, None, None),
        ),
        out_specs=P(every, None),
        check_vma=False,
    )
```

```python
import functools
import math

import jax
import jax.numpy as jnp
from jax import lax
from jax.experimental import pallas as pl
from jax.experimental.pallas import tpu as pltpu
from jax.sharding import Mesh
from jax.sharding import PartitionSpec as P

KVH = 8
WINDOW = 128
SEQ = ("y", "c")
EXP = ("z", "x")


def factors(mesh):
    seq, exp = mesh.shape["seq"], mesh.shape["exp"]
    nc = 2 if seq % 2 == 0 else 1
    nz = 1
    while nz * nz < exp:
        nz *= 2
    return seq // nc, nc, nz, exp // nz


def swapped(value, axis, apart):
    return lax.ppermute(value, axis, [(i, i ^ 1 << apart) for i in range(lax.axis_size(axis))])


def shifted(block, axis, distance):
    devices = range(lax.axis_size(axis))
    route = [(i - distance, i) for i in devices if i - distance in devices]
    return lax.ppermute(block, axis, route)


def rotated(value, axis, by):
    size = lax.axis_size(axis)
    return lax.ppermute(value, axis, [(i, (i + by) % size) for i in range(size)])


def in_plane(value, dy, dx):
    ny, nx = lax.axis_size("y"), lax.axis_size("x")
    route = [
        (y * nx + x, (y + dy) % ny * nx + (x + dx) % nx) for y in range(ny) for x in range(nx)
    ]
    return lax.ppermute(value, ("y", "x"), route)


def attention_kernel(
    window, start_ref, sink_ref, query_ref, key_ref, value_ref, prior_ref, out_ref, keys, values
):
    block = pl.program_id(0)
    width = key_ref.shape[0]
    lanes = keys.shape[1]
    share = lanes // width
    heads = query_ref.shape[1] // width

    @pl.when(block == 0)
    def _():
        scale = 1.0 / math.sqrt(width)
        for half in range(share):
            keys[half] = jnp.zeros(keys.shape[1:], keys.dtype)
            values[half] = jnp.zeros(values.shape[1:], values.dtype)
            at = slice(half * width, (half + 1) * width)
            keys[half, at, :window] = (prior_ref[:width, :] * scale).astype(keys.dtype)
            keys[half, at, window:] = (key_ref[...] * scale).astype(keys.dtype)
            values[half, at, :window] = prior_ref[width:, :]
            values[half, at, window:] = value_ref[...]

    query_pos = lax.broadcasted_iota(jnp.int32, (window, 2 * window), 0)
    key_pos = lax.broadcasted_iota(jnp.int32, (window, 2 * window), 1)
    first = jnp.where((start_ref[0] == 0) & (block == 0), window, 0)
    allowed = (key_pos > query_pos) & (key_pos <= query_pos + window) & (key_pos >= first)
    span = pl.ds(pl.multiple_of(block * window, window), 2 * window)
    for group in range(heads // share):
        at = slice(group * lanes, (group + 1) * lanes)
        query = query_ref[:, at]
        mixed = jnp.zeros((window, lanes), jnp.float32)
        for half in range(share):
            scores = jnp.dot(query, keys[half, :, span], preferred_element_type=jnp.float32)
            scores = jnp.where(allowed, scores, -jnp.inf)
            sink = sink_ref[group * share + half]
            highest = jnp.maximum(jnp.max(scores, axis=1, keepdims=True), sink)
            raised = jnp.exp(scores - highest)
            total = jnp.sum(raised, axis=1, keepdims=True) + jnp.exp(sink - highest)
            probs = (raised * (1.0 / total)).astype(jnp.bfloat16)
            mixed = mixed + lax.dot_general(
                probs, values[half, :, span], (((1,), (1,)), ((), ())),
                preferred_element_type=jnp.float32,
            )
        out_ref[:, at] = mixed.astype(out_ref.dtype)


def window_attention(queries, keys_t, values_t, prior, sinks, start, window):
    rows, columns = queries.shape
    width = keys_t.shape[0]
    lanes = 2 * width

    def whole(array):
        return pl.BlockSpec(array.shape, lambda i: (0, 0))

    return pl.pallas_call(
        functools.partial(attention_kernel, window),
        out_shape=jax.ShapeDtypeStruct(queries.shape, queries.dtype),
        grid=(rows // window,),
        in_specs=[
            pl.BlockSpec(memory_space=pltpu.SMEM),
            pl.BlockSpec(memory_space=pltpu.SMEM),
            pl.BlockSpec((window, columns), lambda i: (i, 0)),
            whole(keys_t),
            whole(values_t),
            whole(prior),
        ],
        out_specs=pl.BlockSpec((window, columns), lambda i: (i, 0)),
        scratch_shapes=[
            pltpu.VMEM((lanes // width, lanes, rows + window), keys_t.dtype),
            pltpu.VMEM((lanes // width, lanes, rows + window), values_t.dtype),
        ],
        name="window_attention",
    )(start, sinks, queries, keys_t, values_t, prior)


def expert_rows(rows_in, gate_up, down_rows):
    hidden_units = gate_up.shape[1] // 2
    both = jnp.dot(rows_in, gate_up, preferred_element_type=jnp.float32)
    gate_part = both[:, :hidden_units]
    up_part = both[:, hidden_units:]
    activated = (gate_part * jax.nn.sigmoid(1.702 * gate_part) * (up_part + 1.0)).astype(
        jnp.bfloat16
    )
    return jnp.dot(activated, down_rows, preferred_element_type=jnp.float32).astype(jnp.bfloat16)


def per_device(
    queries,
    key_rows,
    value_rows,
    sink_logits,
    out_proj,
    residual,
    norm_gain,
    expert_ids,
    gate_weights,
    w_gate_up,
    w_down,
):
    f32, bf16 = jnp.float32, jnp.bfloat16
    ny, nc, nz, nx = (lax.axis_size(a) for a in ("y", "c", "z", "x"))
    yi, ci, zi, xi = (lax.axis_index(a) for a in ("y", "c", "z", "x"))
    seq_index = yi * nc + ci
    exp_index = zi * nx + xi
    local_rows = queries.shape[0]
    width = out_proj.shape[1]
    tokens = local_rows // (nz * nx)
    expert_total = ny * nc * nz * nx
    top_count = expert_ids.shape[1]
    cap = 2 * top_count * tokens // expert_total

    group_devices = nz * nx // KVH
    key_piece = key_rows
    value_piece = value_rows
    for bit_number in range(group_devices.bit_length() - 1):
        other_keys, other_values = swapped((key_piece, value_piece), EXP, bit_number)
        upper_half = jnp.right_shift(exp_index, bit_number) & 1 == 1
        key_piece = jnp.where(
            upper_half,
            jnp.concatenate([other_keys, key_piece], axis=1),
            jnp.concatenate([key_piece, other_keys], axis=1),
        )
        value_piece = jnp.where(
            upper_half,
            jnp.concatenate([other_values, value_piece], axis=1),
            jnp.concatenate([value_piece, other_values], axis=1),
        )
    tail = slice(local_rows - WINDOW, local_rows)
    keys_t, values_t = key_piece.T, value_piece.T
    prior = shifted(jnp.concatenate([keys_t[:, tail], values_t[:, tail]], axis=0), SEQ, 1)

    flat_ids = expert_ids.reshape(-1)
    chosen = (flat_ids[:, None] == jnp.arange(expert_total, dtype=jnp.int32)[None, :]).astype(
        jnp.int32
    )
    slot_rank = jnp.sum((jnp.cumsum(chosen, axis=0) - chosen) * chosen, axis=1)
    slot_index = (flat_ids * cap + slot_rank).reshape(tokens, top_count)
    facts = jnp.concatenate([slot_index.astype(f32), gate_weights], axis=1)
    facts_of = [facts] + [rotated(facts, "z", k) for k in range(1, nz)]

    places = jnp.arange(ny * nx * nc * cap, dtype=jnp.int32)
    rank, rest = places % cap, places // cap
    to_c, rest = (ci + rest % nc) % nc, rest // nc
    to_x, to_y = (xi + rest % nx) % nx, (yi + rest // nx) % ny
    plane_slots = (((to_y * nc + to_c) * nz + zi) * nx + to_x) * cap + rank
    plane_rows = ny * nx * nc * cap

    start = (seq_index * local_rows).reshape(1)
    attended = window_attention(
        queries, keys_t, values_t, prior, sink_logits, start, WINDOW
    )
    partial = jnp.dot(attended, out_proj, preferred_element_type=f32).astype(bf16)

    def rows_of(z, x):
        return lax.dynamic_slice(partial, ((z % nz * nx + x % nx) * tokens, 0), (tokens, width))

    crossed = []
    for step in range(nz):
        block = zi - 1 - step + 2 * nz
        crossed.append(
            [rotated(rows_of(block, xi + dx), "x", dx) for dx in range(1, nx)]
            + [rows_of(block, xi)]
        )
    running = None
    for step in range(nz):
        total = sum(piece.astype(f32) for piece in crossed[step])
        if running is not None:
            total = total + rotated(running, "z", 1).astype(f32)
        running = total.astype(bf16)
    hidden = residual.astype(f32) + total
    scale = lax.rsqrt(jnp.mean(hidden * hidden, axis=-1, keepdims=True) + 1e-05)
    normed = (hidden * scale * norm_gain[None, :]).astype(bf16)

    offsets = [(dy, dx) for dy in range(ny) for dx in range(nx)]
    arriving = normed
    landed = []
    spreads = []
    for k in range(nz):
        if k:
            arriving = rotated(arriving, "z", 1)
        slots = facts_of[k][:, :top_count].astype(jnp.int32)
        hits = plane_slots[None, None, :] == slots[:, :, None]
        spread = jnp.sum(jnp.where(hits, facts_of[k][:, top_count:, None], 0.0), axis=1)
        spreads.append(spread)
        placing = jnp.any(hits, axis=1).astype(bf16)
        placed = lax.dot_general(
            placing, arriving, (((0,), (0,)), ((), ())), preferred_element_type=f32
        ).astype(bf16)
        placed = placed.reshape(ny * nx, nc, cap, width)
        landed.append(
            jnp.stack([placed[0]] + [in_plane(placed[j], *offsets[j]) for j in range(1, ny * nx)])
        )

    groups = [list(range(min(2, nz)))] + [[k] for k in range(2, nz)]
    returned = [None] * nz
    for group in groups:
        mine = jnp.stack([landed[k][:, 0] for k in group])
        given = [mine]
        for dc in range(1, nc):
            given.append(rotated(jnp.stack([landed[k][:, dc] for k in group]), "c", dc))
        rows_in = jnp.stack(given)
        results = expert_rows(rows_in.reshape(-1, width), w_gate_up[0], w_down[0])
        results = results.reshape(rows_in.shape)
        back = [results[0]]
        for dc in range(1, nc):
            back.append(rotated(results[dc], "c", -dc))
        for i, k in enumerate(group):
            returned[k] = jnp.stack([part[i] for part in back], axis=1)

    running = None
    for k in list(range(1, nz)) + [0]:
        rows_back = jnp.stack(
            [returned[k][0]]
            + [in_plane(returned[k][j], -offsets[j][0], -offsets[j][1]) for j in range(1, ny * nx)]
        ).reshape(plane_rows, width)
        high = spreads[k].astype(bf16)
        low = (spreads[k] - high.astype(f32)).astype(bf16)
        total = jnp.dot(high, rows_back, preferred_element_type=f32) + jnp.dot(
            low, rows_back, preferred_element_type=f32
        )
        if running is not None:
            total = total + rotated(running, "z", 1).astype(f32)
        running = total.astype(bf16)
    return (hidden + total).astype(bf16)


def solution(mesh):
    sizes = factors(mesh)
    inner = Mesh(mesh.devices.reshape(sizes), ("y", "c", "z", "x"))
    every = SEQ + EXP

    return jax.shard_map(
        per_device,
        mesh=inner,
        in_specs=(
            P(SEQ, EXP),
            P(SEQ, EXP),
            P(SEQ, EXP),
            P(EXP),
            P(EXP, None),
            P(every, None),
            P(),
            P(every, None),
            P(every, None),
            P(every, None, None),
            P(every, None, None),
        ),
        out_specs=P(every, None),
        check_vma=False,
    )
```
